128 devices in a mesh: dp: 8 (over y, z_lo), mp: 16 (over x, z_hi, core).
Axes of the slice: x: 4, y: 4, z: 4 (z_hi: 2, z_lo: 2; z = z_hi * 2 + z_lo), core: 2. Of those that a mesh axis runs over, the one named last changes fastest.
Arguments:
- tokens: bfloat16 [8192, 8192], P(('dp', 'mp')), may hold values from -6 to 6
- row_counts: int32 [8, 16], replicated, may hold values from 8 to 64, as said below
- gate_blocks: bfloat16 [64, 16, 128, 256], P('mp'), may hold values from -0.125 to 0.125
- gate_index: int32 [64, 16], P('mp'), may hold values from 0 to 63, as said below
- up_blocks: bfloat16 [64, 16, 128, 256], P('mp'), may hold values from -0.125 to 0.125
- up_index: int32 [64, 16], P('mp'), may hold values from 0 to 63, as said below
- down_blocks: bfloat16 [64, 16, 256, 128], P('mp'), may hold values from -0.09375 to 0.09375
- down_index: int32 [64, 16], P('mp'), may hold values from 0 to 63, as said below
Outputs:
- layer_out: bfloat16 [8192, 8192], P(('dp', 'mp'))
The draws below stay inside these ranges and needn't reach their ends.
Inputs may be any that keep to these rules, and one draw needn't show every extreme that they name: `row_counts`: every entry is a multiple of 8; the entries of one column (one mp index) add up to 32 times the number of dp indices, and every column holds one entry equal to 64. `gate_index`: each row holds 16 distinct block rows in increasing order. `up_index`: each row holds 16 distinct block rows in increasing order. `down_index`: each row holds 16 distinct block columns in increasing order.
All inputs are finite; a program needn't handle non-finite values.
Results may differ from the reference program's by a relative error of at most 0.013.
Values may be sent and summed in bfloat16 or wider, within the bound.
No kernel may reach another device: no remote copies, remote signals or barrier semaphores. Data moves between devices by JAX's collectives and lax.ppermute only.
A program may use at most 192 MiB of HBM per device.

```python
import jax
import jax.numpy as jnp
from jax import lax

D = 8192
FF = 16384
NBD = 64
NBF = 64
KNZ = 16
ROWS_IN = 64
BD = 128
BF = 256
BAL = 32
ROWS = 8192
N_DP = 8
N_MP = 16


def pick_blocks(key):
    key_list = jax.random.split(key, NBF)

    def one_column(column_key):
        return jnp.sort(jax.random.permutation(column_key, NBD)[:KNZ])
    return jax.vmap(one_column)(key_list).astype(jnp.int32)


def draw_gate_index(key, part):
    return pick_blocks(jax.random.fold_in(key, 101))


def draw_up_index(key, part):
    return pick_blocks(jax.random.fold_in(key, 202))


def draw_down_index(key, part):
    return pick_blocks(jax.random.fold_in(key, 303))


def draw_row_counts(key, part):
    longest = ROWS_IN // 8
    target = N_DP * ROWS_IN // 16
    spare_units = target - N_DP - longest + 1
    per_device = longest - 1
    slot_total = N_DP * per_device
    owner_ids = jnp.arange(slot_total, dtype=jnp.int32) // per_device
    lane_ids = jnp.arange(N_DP, dtype=jnp.int32)

    def one_lane(lane_key):
        first_key, second_key = jax.random.split(lane_key)
        chosen = jax.random.randint(first_key, (), 0, N_DP)
        scores = jax.random.permutation(second_key, slot_total).astype(jnp.int32)
        scores = jnp.where(owner_ids == chosen, jnp.arange(slot_total, dtype=jnp.int32) - slot_total, scores)
        rank_list = jnp.argsort(jnp.argsort(scores, stable=True), stable=True)
        marked = rank_list < spare_units + per_device
        unit_count = 1 + jnp.sum(((owner_ids[None, :] == lane_ids[:, None]) & marked[None, :]).astype(jnp.int32), axis=1)
        return (8 * unit_count).astype(jnp.int32)
    key_list = jax.random.split(jax.random.fold_in(key, 404), N_MP)
    return jnp.transpose(jax.vmap(one_lane)(key_list)).astype(jnp.int32)


def level_of(rng, shape, shards, smallest, largest):
    factor_of, own = 1.0, jax.random.fold_in(rng, 6)
    for axis_at, blocks in shards:
        draws = jnp.exp(jax.random.uniform(jax.random.fold_in(own, axis_at), (blocks,), jnp.float32, smallest / len(shards), largest / len(shards)))
        factor_of = factor_of * jnp.repeat(draws, shape[axis_at] // blocks).reshape([-1 if axis == axis_at else 1 for axis in range(len(shape))])
    return factor_of


def bell_draw(stream_key, dims, deviation, most, cuts=(), kind=jnp.bfloat16):
    array = jax.random.normal(stream_key, dims, jnp.float32) * deviation
    if len(cuts) > 0:
        array = level_of(stream_key, dims, cuts, -0.22, 0.18) * array
    return jnp.clip(array, min=-most, max=most).astype(kind)


def setup_inputs(seed: int = 0) -> dict:
    splits = jax.random.split(jax.random.key(seed), 9)
    tokens = bell_draw(splits[0], (ROWS, D), 1.0, 6.0, ((0, 128),))
    row_counts = draw_row_counts(jax.random.fold_in(splits[8], 71), 0)
    gate_blocks = bell_draw(splits[2], (NBF, KNZ, BD, BF), (KNZ * BD) ** -0.5, 0.125, ((0, 16),))
    gate_index = draw_gate_index(jax.random.fold_in(splits[8], 71), 0)
    up_blocks = bell_draw(splits[4], (NBF, KNZ, BD, BF), (KNZ * BD) ** -0.5, 0.125, ((0, 16),))
    up_index = draw_up_index(jax.random.fold_in(splits[8], 71), 0)
    down_blocks = bell_draw(splits[6], (NBF, KNZ, BF, BD), (FF * KNZ // NBD) ** -0.5, 0.09375, ((0, 16),))
    down_index = draw_down_index(jax.random.fold_in(splits[8], 71), 0)
    return {"tokens": tokens, "row_counts": row_counts, "gate_blocks": gate_blocks, "gate_index": gate_index, "up_blocks": up_blocks, "up_index": up_index, "down_blocks": down_blocks, "down_index": down_index}


def make_hidden(row_block, gate_blocks, gate_index, up_blocks, up_index):
    row_count = row_block.shape[0]
    split_rows = row_block.reshape(row_count, NBD, BD).astype(jnp.float32)
    gate_input = jnp.take(split_rows, gate_index, axis=1)
    up_input = jnp.take(split_rows, up_index, axis=1)
    gate_value = jnp.einsum("rjkc,jkcn->rjn", gate_input, gate_blocks.astype(jnp.float32), precision=lax.Precision.HIGHEST)
    up_value = jnp.einsum("rjkc,jkcn->rjn", up_input, up_blocks.astype(jnp.float32), precision=lax.Precision.HIGHEST)
    return (jax.nn.silu(gate_value) * up_value).astype(jnp.bfloat16)


def apply_down(hidden, down_blocks, down_index):
    products = jnp.einsum("rjn,jknc->rjkc", hidden.astype(jnp.float32), down_blocks.astype(jnp.float32), precision=lax.Precision.HIGHEST)
    placing = (down_index[:, :, None] == jnp.arange(NBD, dtype=jnp.int32)[None, None, :]).astype(jnp.float32)
    placed = jnp.einsum("rjkc,jkd->rdc", products, placing, precision=lax.Precision.HIGHEST)
    return placed.reshape(hidden.shape[0], D)


def reference(tokens, row_counts, gate_blocks, gate_index, up_blocks, up_index, down_blocks, down_index):
    per_shard = NBF // N_MP

    def one_block(row_block):
        running = jnp.zeros((row_block.shape[0], D), jnp.float32)
        for shard_id in range(N_MP):
            low_block = shard_id * per_shard
            high_block = low_block + per_shard
            hidden = make_hidden(row_block, gate_blocks[low_block:high_block], gate_index[low_block:high_block],
                                 up_blocks[low_block:high_block], up_index[low_block:high_block])
            partial_sum = apply_down(hidden, down_blocks[low_block:high_block], down_index[low_block:high_block]).astype(jnp.bfloat16)
            running = running + lax.optimization_barrier(partial_sum).astype(jnp.float32)
        return running

    row_ids = jnp.arange(ROWS, dtype=jnp.int32)
    device_of = row_ids // ROWS_IN
    row_limit = jnp.take(row_counts.reshape(-1), device_of)
    valid_mask = (row_ids % ROWS_IN) < row_limit
    valid_total = BAL * N_DP * N_MP
    valid_ids = jnp.nonzero(valid_mask, size=valid_total)[0].astype(jnp.int32)
    compact = jnp.take(tokens, valid_ids, axis=0)
    block_rows = 256
    results = lax.map(one_block, compact.reshape(valid_total // block_rows, block_rows, D)).reshape(valid_total, D)
    layer_out = jnp.zeros((ROWS, D), jnp.float32).at[valid_ids].set(results)
    return layer_out.astype(jnp.bfloat16)
```

```python
import functools

import jax
import jax.numpy as jnp
from jax import lax
from jax.experimental import pallas as pl
from jax.experimental.pallas import tpu as pltpu
from jax.sharding import PartitionSpec as P


NX = 4
MP = [(x, z, c) for x in range(NX) for z in range(2) for c in range(2)]


def mp_index(x, z, c):
    return (x % NX) * 4 + (z % 2) * 2 + (c % 2)


def shift_pairs(dx, dz, dc):
    return [(mp_index(x, z, c), mp_index(x + dx, z + dz, c + dc)) for x, z, c in MP]


def shift(value, dx=0, dz=0, dc=0):
    return lax.ppermute(value, "mp", shift_pairs(dx, dz, dc))


def gather_parts(part_p, part_q):
    blocks_p, blocks_q = {}, {}
    q = part_q
    blocks_p[0, 0] = part_p
    blocks_q[0, 0] = q
    blocks_p[0, 1] = shift(part_p, dz=1)
    blocks_q[3, 0] = shift(q, dx=1)
    blocks_q[1, 0] = shift(q, dx=-1)
    blocks_q[2, 0] = shift(q, dx=2)
    for dz in range(2):
        blocks_p[3, dz] = shift(blocks_p[0, dz], dx=1)
        blocks_p[1, dz] = shift(blocks_p[0, dz], dx=-1)
    blocks_p[2, 0] = shift(blocks_p[3, 0], dx=1)
    blocks_p[2, 1] = shift(blocks_p[1, 1], dx=-1)
    for dx in (0, 1, 3, 2):
        blocks_q[dx, 1] = shift(blocks_q[dx, 0], dz=1)
    return blocks_p, blocks_q


ORDER = [(dx, dz) for dx in range(NX) for dz in range(2)]


def layer_kernel(rows, width_p, width_q, nonzero, own_columns,
                 gate_index, up_index, down_index,
                 gate_own, gate_other, up_own, up_other, down_own, down_other, *rest):
    pieces = rest[:16]
    far_0, far_1, next_1, next_3, own_0, cross_1, cross_0 = rest[16:23]
    x_all, left, total, sems = rest[23:]
    step = pl.program_id(0)
    block_width = gate_own.shape[2]
    unit_width = gate_own.shape[3]

    @pl.when(step == 0)
    def _():
        copies = []
        for at in range(8):
            copies.append(pltpu.make_async_copy(
                pieces[at], x_all.at[pl.ds(at * rows, rows), pl.ds(0, width_p)], sems.at[at]))
            copies.append(pltpu.make_async_copy(
                pieces[8 + at], x_all.at[pl.ds(at * rows, rows), pl.ds(width_p, width_q)], sems.at[8 + at]))
        for copy in copies:
            copy.start()
        total[...] = jnp.zeros_like(total)
        for copy in copies:
            copy.wait()

    def run(gate_ref, up_ref, down_ref):
        def project(index, weights):
            for k in range(nonzero):
                at = pl.multiple_of(index[step, k] * block_width, block_width)
                left[:, k * block_width:(k + 1) * block_width] = x_all[:, pl.ds(at, block_width)]
            return jnp.dot(left[...], weights[0].reshape(nonzero * block_width, unit_width),
                           preferred_element_type=jnp.float32)

        gate = project(gate_index, gate_ref)
        up = project(up_index, up_ref)
        hidden = (gate / (1.0 + jnp.exp(-gate)) * up).astype(jnp.bfloat16)
        for k in range(0, nonzero, 2):
            pair = jnp.concatenate([down_ref[0, k], down_ref[0, k + 1]], axis=1)
            value = jnp.dot(hidden, pair, preferred_element_type=jnp.float32)
            for i in range(2):
                at = pl.multiple_of(down_index[step, k + i] * block_width, block_width)
                total[:, pl.ds(at, block_width)] += value[:, i * block_width:(i + 1) * block_width]

    @pl.when(step < own_columns)
    def _():
        run(gate_own, up_own, down_own)

    @pl.when(step >= own_columns)
    def _():
        run(gate_other, up_other, down_other)

    @pl.when(step == 2 * own_columns - 1)
    def _():
        def block(dx, dz, part):
            at = ORDER.index((dx, dz)) * rows
            if part == 0:
                return total[at:at + rows, :width_p].astype(jnp.bfloat16)
            return total[at:at + rows, width_p:].astype(jnp.bfloat16)

        far_0[...] = block(2, 0, 0)
        far_1[...] = block(2, 1, 0)
        for dz in range(2):
            next_1[dz * rows:(dz + 1) * rows, :] = block(1, dz, 0)
            next_3[dz * rows:(dz + 1) * rows, :] = block(3, dz, 0)
            own_0[dz * rows:(dz + 1) * rows, :] = block(0, dz, 0)
        for dx in range(NX):
            cross_1[dx * rows:(dx + 1) * rows, :] = block(dx, 1, 1)
            cross_0[dx * rows:(dx + 1) * rows, :] = block(dx, 0, 1)


def run_layer(blocks_p, blocks_q, index_own, index_other, weights_own, weights_other):
    rows, width_p = blocks_p[0, 0].shape
    width_q = blocks_q[0, 0].shape[1]
    width = width_p + width_q
    own_columns, nonzero, block_width, unit_width = weights_own[0].shape
    tables = [jnp.concatenate([a, b], axis=0) for a, b in zip(index_own, index_other)]

    def own_map(j, *_):
        return (jnp.minimum(j, own_columns - 1), 0, 0, 0)

    def other_map(j, *_):
        return (jnp.maximum(j - own_columns, 0), 0, 0, 0)

    weight_specs, weights = [], []
    for own, other in zip(weights_own, weights_other):
        shape = (1,) + own.shape[1:]
        weight_specs += [pl.BlockSpec(shape, own_map), pl.BlockSpec(shape, other_map)]
        weights += [own, other]
    pieces = [blocks_p[key] for key in ORDER] + [blocks_q[key] for key in ORDER]
    out_shapes = [(rows, width_p)] * 2 + [(2 * rows, width_p)] * 3 + [(4 * rows, width_q)] * 2
    kernel = functools.partial(layer_kernel, rows, width_p, width_q, nonzero, own_columns)
    return pl.pallas_call(
        kernel,
        grid_spec=pltpu.PrefetchScalarGridSpec(
            num_scalar_prefetch=3,
            grid=(2 * own_columns,),
            in_specs=weight_specs + [pl.BlockSpec(memory_space=pl.ANY)] * 16,
            out_specs=[pl.BlockSpec(s, lambda j, *_: (0, 0)) for s in out_shapes],
            scratch_shapes=[
                pltpu.VMEM((8 * rows, width), jnp.bfloat16),
                pltpu.VMEM((8 * rows, nonzero * block_width), jnp.bfloat16),
                pltpu.VMEM((8 * rows, width), jnp.float32),
                pltpu.SemaphoreType.DMA((16,)),
            ],
        ),
        out_shape=[jax.ShapeDtypeStruct(s, jnp.bfloat16) for s in out_shapes],
        compiler_params=pltpu.CompilerParams(
            dimension_semantics=("arbitrary",), vmem_limit_bytes=58 * 1024 * 1024),
        name="sparse_ffn",
    )(*tables, *weights, *pieces)


def wide(value):
    return value.astype(jnp.float32)


def narrow(value):
    return value.astype(jnp.bfloat16)


def scatter_parts(sums):
    far_0, far_1, next_1, next_3, own_0, cross_1, cross_0 = sums
    rows = far_0.shape[0]
    got_cross = shift(cross_1, dz=1)
    got_0 = shift(far_0, dx=1)
    got_1 = shift(far_1, dx=-1)
    to_1 = jnp.concatenate([narrow(wide(next_1[:rows]) + wide(got_0)), next_1[rows:]], axis=0)
    to_3 = jnp.concatenate([next_3[:rows], narrow(wide(next_3[rows:]) + wide(got_1))], axis=0)
    got_left = shift(to_1, dx=1)
    got_right = shift(to_3, dx=-1)
    met = wide(own_0) + wide(got_left) + wide(got_right)
    got_z = shift(narrow(met[rows:]), dz=1)
    part_p = met[:rows] + wide(got_z)
    crossed = [wide(cross_0[i * rows:(i + 1) * rows]) + wide(got_cross[i * rows:(i + 1) * rows]) for i in range(NX)]
    part_q = crossed[0] + wide(shift(narrow(crossed[1]), dx=1)) + wide(shift(narrow(crossed[3]), dx=-1)) \
        + wide(shift(narrow(crossed[2]), dx=2))
    return jnp.concatenate([part_p, part_q], axis=1)


def body(tokens, row_counts, gate_blocks, gate_index, up_blocks, up_index, down_blocks, down_index):
    own_dp = lax.axis_index("dp")
    own_mp = lax.axis_index("mp")
    rows, width = tokens.shape
    block_width = gate_blocks.shape[2]
    width_p = (width // block_width * 9 // 16) * block_width
    index_own = (gate_index, up_index, down_index)
    index_both = shift(jnp.stack(index_own), dc=1)
    index_other = (index_both[0], index_both[1], index_both[2])
    weights_own = (gate_blocks, up_blocks, down_blocks)
    weights_other = tuple(shift(w, dc=1) for w in weights_own)
    blocks_p, blocks_q = gather_parts(tokens[:, :width_p], tokens[:, width_p:])
    sums = run_layer(blocks_p, blocks_q, index_own, index_other, weights_own, weights_other)
    summed = scatter_parts(sums)
    valid_rows = jnp.arange(rows, dtype=jnp.int32) < row_counts[own_dp, own_mp]
    return jnp.where(valid_rows[:, None], summed, 0.0).astype(jnp.bfloat16)


def solution(mesh):
    in_specs = (
        P(("dp", "mp"), None),
        P(),
        P("mp", None, None, None),
        P("mp", None),
        P("mp", None, None, None),
        P("mp", None),
        P("mp", None, None, None),
        P("mp", None),
    )
    out_specs = P(("dp", "mp"), None)
    return jax.shard_map(body, mesh=mesh, in_specs=in_specs, out_specs=out_specs, check_vma=False)
```

```python
import functools

import jax
import jax.numpy as jnp
from jax import lax
from jax.experimental import pallas as pl
from jax.experimental.pallas import tpu as pltpu
from jax.sharding import PartitionSpec as P


NX = 4
MP = [(x, z, c) for x in range(NX) for z in range(2) for c in range(2)]


def mp_index(x, z, c):
    return (x % NX) * 4 + (z % 2) * 2 + (c % 2)


def shift_pairs(dx, dz, dc):
    return [(mp_index(x, z, c), mp_index(x + dx, z + dz, c + dc)) for x, z, c in MP]


def shift(value, name, dx=0, dz=0, dc=0):
    with jax.named_scope(name):
        return lax.ppermute(value, "mp", shift_pairs(dx, dz, dc))


def gather_parts(part_p, part_q):
    rows = part_p.shape[0]
    p_cross = shift(part_p, "p_cross", dz=1)
    q_left = shift(part_q, "q_left", dx=1)
    q_right = shift(part_q, "q_right", dx=-1)
    q_far = shift(part_q, "q_far", dx=2)
    q_cross = shift(part_q, "q_cross", dz=1)
    p_pair = jnp.concatenate([part_p, p_cross], axis=0)
    p_left = shift(p_pair, "p_left", dx=1)
    p_right = shift(p_pair, "p_right", dx=-1)
    q_three = jnp.concatenate([q_left, q_right, q_far], axis=0)
    q_three_cross = shift(q_three, "q_three_cross", dz=1)
    p_far_0 = shift(p_left[:rows], "p_far_0", dx=1)
    p_far_1 = shift(p_right[rows:], "p_far_1", dx=-1)
    arrays = [p_pair, p_left, p_right, p_far_0, p_far_1, part_q, q_three, q_cross, q_three_cross]
    places = [
        (0, 0, [(0, 0), (0, 1)]), (1, 0, [(3, 0), (3, 1)]), (2, 0, [(1, 0), (1, 1)]), (3, 0, [(2, 0)]), (4, 0, [(2, 1)]),
        (5, 1, [(0, 0)]), (6, 1, [(3, 0), (1, 0), (2, 0)]), (7, 1, [(0, 1)]), (8, 1, [(3, 1), (1, 1), (2, 1)]),
    ]
    return arrays, places


ORDER = [(dx, dz) for dx in range(NX) for dz in range(2)]


def layer_kernel(places, rows, width_p, width_q, nonzero, own_columns,
                 gate_index, up_index, down_index,
                 gate_own, gate_other, up_own, up_other, down_own, down_other, *rest):
    pieces = rest[:len(places)]
    far_0, far_1, next_1, next_3, own_0, cross_1, cross_0 = rest[len(places):len(places) + 7]
    x_all, left, total = rest[len(places) + 7:]
    step = pl.program_id(0)
    block_width = gate_own.shape[2]
    unit_width = gate_own.shape[3]

    @pl.when(step == 0)
    def _():
        for which, part, keys in places:
            for i, key in enumerate(keys):
                at = ORDER.index(key) * rows
                columns = slice(0, width_p) if part == 0 else slice(width_p, width_p + width_q)
                x_all[at:at + rows, columns] = pieces[which][i * rows:(i + 1) * rows, :]
        total[...] = jnp.zeros_like(total)

    def run(gate_ref, up_ref, down_ref):
        def project(index, weights):
            for k in range(nonzero):
                at = pl.multiple_of(index[step, k] * block_width, block_width)
                left[:, k * block_width:(k + 1) * block_width] = x_all[:, pl.ds(at, block_width)]
            return jnp.dot(left[...], weights[0].reshape(nonzero * block_width, unit_width),
                           preferred_element_type=jnp.float32)

        gate = project(gate_index, gate_ref)
        up = project(up_index, up_ref)
        hidden = (gate / (1.0 + jnp.exp(-gate)) * up).astype(jnp.bfloat16)
        for k in range(0, nonzero, 2):
            pair = jnp.concatenate([down_ref[0, k], down_ref[0, k + 1]], axis=1)
            value = jnp.dot(hidden, pair, preferred_element_type=jnp.float32)
            for i in range(2):
                at = pl.multiple_of(down_index[step, k + i] * block_width, block_width)
                total[:, pl.ds(at, block_width)] += value[:, i * block_width:(i + 1) * block_width]

    @pl.when(step < own_columns)
    def _():
        run(gate_own, up_own, down_own)

    @pl.when(step >= own_columns)
    def _():
        run(gate_other, up_other, down_other)

    @pl.when(step == 2 * own_columns - 1)
    def _():
        def block(dx, dz, part):
            at = ORDER.index((dx, dz)) * rows
            if part == 0:
                return total[at:at + rows, :width_p].astype(jnp.bfloat16)
            return total[at:at + rows, width_p:].astype(jnp.bfloat16)

        far_0[...] = block(2, 0, 0)
        far_1[...] = block(2, 1, 0)
        for dz in range(2):
            next_1[dz * rows:(dz + 1) * rows, :] = block(1, dz, 0)
            next_3[dz * rows:(dz + 1) * rows, :] = block(3, dz, 0)
            own_0[dz * rows:(dz + 1) * rows, :] = block(0, dz, 0)
        for dx in range(NX):
            cross_1[dx * rows:(dx + 1) * rows, :] = block(dx, 1, 1)
            cross_0[dx * rows:(dx + 1) * rows, :] = block(dx, 0, 1)


def run_layer(pieces, places, rows, index_own, index_other, weights_own, weights_other):
    width_p = pieces[0].shape[1]
    width_q = pieces[-1].shape[1]
    width = width_p + width_q
    own_columns, nonzero, block_width, unit_width = weights_own[0].shape
    tables = [jnp.concatenate([a, b], axis=0) for a, b in zip(index_own, index_other)]

    def own_map(j, *_):
        return (jnp.minimum(j, own_columns - 1), 0, 0, 0)

    def other_map(j, *_):
        return (jnp.maximum(j - own_columns, 0), 0, 0, 0)

    weight_specs, weights = [], []
    for own, other in zip(weights_own, weights_other):
        shape = (1,) + own.shape[1:]
        weight_specs += [pl.BlockSpec(shape, own_map), pl.BlockSpec(shape, other_map)]
        weights += [own, other]
    out_shapes = [(rows, width_p)] * 2 + [(2 * rows, width_p)] * 3 + [(4 * rows, width_q)] * 2
    kernel = functools.partial(layer_kernel, places, rows, width_p, width_q, nonzero, own_columns)
    return pl.pallas_call(
        kernel,
        grid_spec=pltpu.PrefetchScalarGridSpec(
            num_scalar_prefetch=3,
            grid=(2 * own_columns,),
            in_specs=weight_specs + [pl.BlockSpec(memory_space=pltpu.VMEM)] * len(pieces),
            out_specs=[pl.BlockSpec(memory_space=pltpu.VMEM)] * len(out_shapes),
            scratch_shapes=[
                pltpu.VMEM((8 * rows, width), jnp.bfloat16),
                pltpu.VMEM((8 * rows, nonzero * block_width), jnp.bfloat16),
                pltpu.VMEM((8 * rows, width), jnp.float32),
            ],
        ),
        out_shape=[jax.ShapeDtypeStruct(s, jnp.bfloat16) for s in out_shapes],
        compiler_params=pltpu.CompilerParams(
            dimension_semantics=("arbitrary",), vmem_limit_bytes=40 * 1024 * 1024),
        name="sparse_ffn",
    )(*tables, *weights, *pieces)


def wide(value):
    return value.astype(jnp.float32)


def narrow(value):
    return value.astype(jnp.bfloat16)


def scatter_parts(sums):
    far_0, far_1, next_1, next_3, own_0, cross_1, cross_0 = sums
    rows = far_0.shape[0]
    got_cross = shift(cross_1, "s_cross", dz=1)
    got_0 = shift(far_0, "s_far_0", dx=1)
    got_1 = shift(far_1, "s_far_1", dx=-1)
    to_1 = jnp.concatenate([narrow(wide(next_1[:rows]) + wide(got_0)), next_1[rows:]], axis=0)
    to_3 = jnp.concatenate([next_3[:rows], narrow(wide(next_3[rows:]) + wide(got_1))], axis=0)
    got_left = shift(to_1, "s_left", dx=1)
    got_right = shift(to_3, "s_right", dx=-1)
    met = wide(own_0) + wide(got_left) + wide(got_right)
    got_z = shift(narrow(met[rows:]), "s_own_cross", dz=1)
    part_p = met[:rows] + wide(got_z)
    crossed = [wide(cross_0[i * rows:(i + 1) * rows]) + wide(got_cross[i * rows:(i + 1) * rows]) for i in range(NX)]
    part_q = crossed[0] + wide(shift(narrow(crossed[1]), "s_q_left", dx=1)) + wide(shift(narrow(crossed[3]), "s_q_right", dx=-1)) \
        + wide(shift(narrow(crossed[2]), "s_q_far", dx=2))
    return narrow(part_p), narrow(part_q)


UNIT = 8


def copy_units(sources, index, out_widths, count=None):
    units = index.shape[0]
    in_starts = [sum(s.shape[1] for s in sources[:i]) for i in range(len(sources))]
    out_starts = [sum(out_widths[:i]) for i in range(len(out_widths))]
    spans = []
    for i, source in enumerate(sources):
        for o, width in enumerate(out_widths):
            low = max(in_starts[i], out_starts[o])
            high = min(in_starts[i] + source.shape[1], out_starts[o] + width)
            if low < high:
                spans.append((i, low - in_starts[i], o, low - out_starts[o], high - low))

    def kernel(table, *refs):
        ins, outs = refs[:len(sources)], refs[len(sources):]
        for unit in range(units):
            start = pl.multiple_of(table[unit] * UNIT, UNIT)
            for i, from_column, o, to_column, width in spans:
                value = ins[i][pl.ds(start, UNIT), from_column:from_column + width]
                if count is not None:
                    value = jnp.where(unit < table[units], value, jnp.zeros_like(value))
                outs[o][unit * UNIT:(unit + 1) * UNIT, to_column:to_column + width] = value

    table = index if count is None else jnp.concatenate([index, count[None]])
    return pl.pallas_call(
        kernel,
        in_specs=[pl.BlockSpec(memory_space=pltpu.SMEM)] + [pl.BlockSpec(memory_space=pltpu.VMEM)] * len(sources),
        out_specs=[pl.BlockSpec(memory_space=pltpu.VMEM)] * len(out_widths),
        out_shape=[jax.ShapeDtypeStruct((units * UNIT, w), jnp.bfloat16) for w in out_widths],
        compiler_params=pltpu.CompilerParams(vmem_limit_bytes=8 * 1024 * 1024),
        name="copy_units",
    )(table, *sources)


def plan(row_counts, own_dp, own_mp):
    n_dp = row_counts.shape[0]
    counts = lax.dynamic_slice_in_dim(row_counts, own_mp, 1, axis=1)[:, 0] // UNIT
    ends = jnp.cumsum(counts)
    firsts = ends - counts
    ids = jnp.arange(n_dp, dtype=jnp.int32)
    own_first = lax.dynamic_index_in_dim(firsts, own_dp, keepdims=False)
    own_count = lax.dynamic_index_in_dim(counts, own_dp, keepdims=False)
    send = (ids - own_first) % n_dp
    return n_dp, firsts, ends, ids, own_first, own_count, send


def body(tokens, row_counts, gate_blocks, gate_index, up_blocks, up_index, down_blocks, down_index):
    own_dp = lax.axis_index("dp")
    own_mp = lax.axis_index("mp")
    rows, width = tokens.shape
    block_width = gate_blocks.shape[2]
    width_p = (width // block_width * 9 // 16) * block_width
    n_dp, firsts, ends, ids, own_first, own_count, send = plan(row_counts, own_dp, own_mp)
    kept_units = rows // UNIT // 2
    numbers = jnp.arange(kept_units, dtype=jnp.int32) * n_dp + own_dp
    source_of = jnp.sum((ends[None, :] <= numbers[:, None]).astype(jnp.int32), axis=1)
    back = jnp.clip((firsts + (own_dp - firsts) % n_dp) // n_dp, 0, kept_units - 1)
    index_own = (gate_index, up_index, down_index)
    index_both = shift(jnp.stack(index_own), "w_index", dc=1)
    index_other = (index_both[0], index_both[1], index_both[2])
    weights_own = (gate_blocks, up_blocks, down_blocks)
    weights_other = tuple(shift(w, "w_blocks", dc=1) for w in weights_own)
    rolled, = copy_units([tokens], send, [width])
    spread = lax.all_to_all(rolled, "dp", split_axis=0, concat_axis=0, tiled=True)
    kept = kept_units * UNIT
    part_p, part_q = copy_units([spread], source_of, [width_p, width - width_p])
    pieces, places = gather_parts(part_p, part_q)
    sums = run_layer(pieces, places, kept, index_own, index_other, weights_own, weights_other)
    part_p, part_q = scatter_parts(sums)
    returned, = copy_units([part_p, part_q], back, [width])
    received = lax.all_to_all(returned, "dp", split_axis=0, concat_axis=0, tiled=True)
    restored, = copy_units([received], (own_first + ids) % n_dp, [width], own_count)
    return restored


def solution(mesh):
    in_specs = (
        P(("dp", "mp"), None),
        P(),
        P("mp", None, None, None),
        P("mp", None),
        P("mp", None, None, None),
        P("mp", None),
        P("mp", None, None, None),
        P("mp", None),
    )
    out_specs = P(("dp", "mp"), None)
    return jax.shard_map(body, mesh=mesh, in_specs=in_specs, out_specs=out_specs, check_vma=False)
```

```python
import functools

import jax
import jax.numpy as jnp
from jax import lax
from jax.experimental import pallas as pl
from jax.experimental.pallas import tpu as pltpu
from jax.sharding import PartitionSpec as P


NX = 4
MP = [(x, z, c) for x in range(NX) for z in range(2) for c in range(2)]


def mp_index(x, z, c):
    return (x % NX) * 4 + (z % 2) * 2 + (c % 2)


def shift_pairs(dx, dz, dc):
    return [(mp_index(x, z, c), mp_index(x + dx, z + dz, c + dc)) for x, z, c in MP]


def shift(value, dx=0, dz=0, dc=0):
    return lax.ppermute(value, "mp", shift_pairs(dx, dz, dc))


ORDER = [(dx, dz) for dx in range(NX) for dz in range(2)]


def gather_z_first(part):
    cross = shift(part, dz=1)
    pair = jnp.concatenate([part, cross], axis=0)
    left = shift(pair, dx=1)
    right = shift(pair, dx=-1)
    far = shift(pair, dx=2)
    return [(pair, [(0, 0), (0, 1)]), (left, [(3, 0), (3, 1)]), (right, [(1, 0), (1, 1)]), (far, [(2, 0), (2, 1)])]


def gather_x_first(part):
    left = shift(part, dx=1)
    right = shift(part, dx=-1)
    far = shift(part, dx=2)
    cross = shift(part, dz=1)
    three = jnp.concatenate([left, right, far], axis=0)
    three_cross = shift(three, dz=1)
    return [(part, [(0, 0)]), (three, [(3, 0), (1, 0), (2, 0)]),
            (cross, [(0, 1)]), (three_cross, [(3, 1), (1, 1), (2, 1)])]


Z_LAST = [[(2, 0)], [(2, 1)], [(1, 0), (1, 1)], [(3, 0), (3, 1)], [(0, 0), (0, 1)]]
Z_LAST_DIRECT = [[(dx, 0), (dx, 1)] for dx in (2, 1, 3, 0)]
Z_FIRST = [[(dx, 1) for dx in range(NX)], [(dx, 0) for dx in range(NX)]]


def layer_kernel(loads, stores, nonzero, own_columns,
                 gate_index, up_index, down_index,
                 gate_own, gate_other, up_own, up_other, down_own, down_other, *rest):
    n_in, n_out = 1 + max(p[0] for p in loads), 1 + max(p[0] for p in stores)
    pieces, outs = rest[:n_in], rest[n_in:n_in + n_out]
    x_all, gate_left, up_left, total = rest[n_in + n_out:]
    step = pl.program_id(0)
    block_width = gate_own.shape[2]
    unit_width = gate_own.shape[3]

    @pl.when(step == 0)
    def _():
        for which, piece_row, rows, row, column, width in loads:
            x_all[row:row + rows, column:column + width] = pieces[which][piece_row:piece_row + rows, :]
        total[...] = jnp.zeros_like(total)

    def run(gate_ref, up_ref, down_ref):
        def project(index, weights, left):
            for k in range(nonzero):
                at = pl.multiple_of(index[step, k] * block_width, block_width)
                left[:, k * block_width:(k + 1) * block_width] = x_all[:, pl.ds(at, block_width)]
            return jnp.dot(left[...], weights[0].reshape(nonzero * block_width, unit_width),
                           preferred_element_type=jnp.float32)

        gate = project(gate_index, gate_ref, gate_left)
        up = project(up_index, up_ref, up_left)
        hidden = (gate / (1.0 + jnp.exp(-gate)) * up).astype(jnp.bfloat16)
        for k in range(0, nonzero, 2):
            pair = jnp.concatenate([down_ref[0, k], down_ref[0, k + 1]], axis=1)
            value = jnp.dot(hidden, pair, preferred_element_type=jnp.float32)
            for i in range(2):
                at = pl.multiple_of(down_index[step, k + i] * block_width, block_width)
                total[:, pl.ds(at, block_width)] += value[:, i * block_width:(i + 1) * block_width]

    @pl.when(step < own_columns)
    def _():
        run(gate_own, up_own, down_own)

    @pl.when(step >= own_columns)
    def _():
        run(gate_other, up_other, down_other)

    @pl.when(step == 2 * own_columns - 1)
    def _():
        for which, out_row, rows, row, column, width in stores:
            outs[which][out_row:out_row + rows, :] = total[row:row + rows, column:column + width].astype(jnp.bfloat16)


def run_layer(gathered_parts, sent_parts, width, index_own, index_other, weights_own, weights_other):
    loads, stores, pieces, out_shapes, all_rows = [], [], [], [], 0
    for gathered, rows, row, column in gathered_parts:
        all_rows = max(all_rows, row + 8 * rows)
        for array, keys in gathered:
            for i, key in enumerate(keys):
                loads.append((len(pieces), i * rows, rows, row + ORDER.index(key) * rows, column, array.shape[1]))
            pieces.append(array)
    for sends, rows, row, column, part_width in sent_parts:
        for keys in sends:
            for i, key in enumerate(keys):
                stores.append((len(out_shapes), i * rows, rows, row + ORDER.index(key) * rows, column, part_width))
            out_shapes.append((len(keys) * rows, part_width))
    own_columns, nonzero, block_width, _ = weights_own[0].shape
    tables = [jnp.concatenate([a, b], axis=0) for a, b in zip(index_own, index_other)]

    def own_map(j, *_):
        return (jnp.minimum(j, own_columns - 1), 0, 0, 0)

    def other_map(j, *_):
        return (jnp.maximum(j - own_columns, 0), 0, 0, 0)

    weight_specs, weights = [], []
    for own, other in zip(weights_own, weights_other):
        shape = (1,) + own.shape[1:]
        weight_specs += [pl.BlockSpec(shape, own_map), pl.BlockSpec(shape, other_map)]
        weights += [own, other]
    sums = pl.pallas_call(
        functools.partial(layer_kernel, loads, stores, nonzero, own_columns),
        grid_spec=pltpu.PrefetchScalarGridSpec(
            num_scalar_prefetch=3,
            grid=(2 * own_columns,),
            in_specs=weight_specs + [pl.BlockSpec(memory_space=pltpu.VMEM)] * len(pieces),
            out_specs=[pl.BlockSpec(memory_space=pltpu.VMEM)] * len(out_shapes),
            scratch_shapes=[
                pltpu.VMEM((all_rows, width), jnp.bfloat16),
                pltpu.VMEM((all_rows, nonzero * block_width), jnp.bfloat16),
                pltpu.VMEM((all_rows, nonzero * block_width), jnp.bfloat16),
                pltpu.VMEM((all_rows, width), jnp.float32),
            ],
        ),
        out_shape=[jax.ShapeDtypeStruct(s, jnp.bfloat16) for s in out_shapes],
        compiler_params=pltpu.CompilerParams(
            dimension_semantics=("arbitrary",), vmem_limit_bytes=45 * 1024 * 1024),
        name="sparse_ffn",
    )(*tables, *weights, *pieces)
    split, at = [], 0
    for sends, *_ in sent_parts:
        split.append(sums[at:at + len(sends)])
        at += len(sends)
    return split


def wide(value):
    return value.astype(jnp.float32)


def narrow(value):
    return value.astype(jnp.bfloat16)


def scatter_z_last(sums):
    far_0, far_1, next_1, next_3, own = sums
    rows = far_0.shape[0]
    got_0 = shift(far_0, dx=1)
    got_1 = shift(far_1, dx=-1)
    to_1 = jnp.concatenate([narrow(wide(next_1[:rows]) + wide(got_0)), next_1[rows:]], axis=0)
    to_3 = jnp.concatenate([next_3[:rows], narrow(wide(next_3[rows:]) + wide(got_1))], axis=0)
    got_left = shift(to_1, dx=1)
    got_right = shift(to_3, dx=-1)
    met = wide(own) + wide(got_left) + wide(got_right)
    got_z = shift(narrow(met[rows:]), dz=1)
    return narrow(met[:rows] + wide(got_z))


def scatter_z_last_direct(sums):
    far, next_1, next_3, own = sums
    rows = far.shape[0] // 2
    got = [shift(far, dx=2), shift(next_1, dx=1), shift(next_3, dx=-1)]
    met = wide(own) + wide(got[0]) + wide(got[1]) + wide(got[2])
    got_z = shift(narrow(met[rows:]), dz=1)
    return narrow(met[:rows] + wide(got_z))


def scatter_z_first(sums):
    cross_1, cross_0 = sums
    rows = cross_1.shape[0] // NX
    got_cross = shift(cross_1, dz=1)
    met = [wide(cross_0[i * rows:(i + 1) * rows]) + wide(got_cross[i * rows:(i + 1) * rows]) for i in range(NX)]
    return narrow(met[0] + wide(shift(narrow(met[1]), dx=1))
                  + wide(shift(narrow(met[3]), dx=-1))
                  + wide(shift(narrow(met[2]), dx=2)))


UNIT = 8


def copy_units(sources, index, out_widths, head=None, count=None):
    units = index.shape[0]
    in_starts = [sum(s.shape[1] for s in sources[:i]) for i in range(len(sources))]
    out_starts = [sum(out_widths[:i]) for i in range(len(out_widths))]
    spans = []
    for i, source in enumerate(sources):
        for o, width in enumerate(out_widths):
            low = max(in_starts[i], out_starts[o])
            high = min(in_starts[i] + source.shape[1], out_starts[o] + width)
            if low < high:
                spans.append((i, low - in_starts[i], o, low - out_starts[o], high - low))
    ins_all = list(sources) if head is None else [*sources, head]
    table = index if head is None else jnp.concatenate([index, count[None]])

    def kernel(table, *refs):
        ins, outs = refs[:len(sources)], refs[len(ins_all):]
        for unit in range(units):
            start = pl.multiple_of(table[unit] * UNIT, UNIT)
            for i, from_column, o, to_column, width in spans:
                if head is not None and unit == 0:
                    value = refs[len(sources)][...]
                else:
                    value = ins[i][pl.ds(start, UNIT), from_column:from_column + width]
                    if head is not None:
                        value = jnp.where(unit < table[units], value, jnp.zeros_like(value))
                outs[o][unit * UNIT:(unit + 1) * UNIT, to_column:to_column + width] = value

    return pl.pallas_call(
        kernel,
        in_specs=[pl.BlockSpec(memory_space=pltpu.SMEM)] + [pl.BlockSpec(memory_space=pltpu.VMEM)] * len(ins_all),
        out_specs=[pl.BlockSpec(memory_space=pltpu.VMEM)] * len(out_widths),
        out_shape=[jax.ShapeDtypeStruct((units * UNIT, w), jnp.bfloat16) for w in out_widths],
        compiler_params=pltpu.CompilerParams(vmem_limit_bytes=8 * 1024 * 1024),
        name="copy_units",
    )(table, *ins_all)


def plan(row_counts, own_dp, own_mp):
    n_dp = row_counts.shape[0]
    counts = lax.dynamic_slice_in_dim(row_counts, own_mp, 1, axis=1)[:, 0] // UNIT - 1
    ends = jnp.cumsum(counts)
    firsts = ends - counts
    ids = jnp.arange(n_dp, dtype=jnp.int32)
    own_first = lax.dynamic_index_in_dim(firsts, own_dp, keepdims=False)
    own_count = lax.dynamic_index_in_dim(counts, own_dp, keepdims=False)
    return n_dp, firsts, ends, ids, own_first, own_count


def run(tokens, row_counts, gate_blocks, gate_index, up_blocks, up_index, down_blocks, down_index):
    own_dp = lax.axis_index("dp")
    own_mp = lax.axis_index("mp")
    rows, width = tokens.shape
    block_width = gate_blocks.shape[2]
    width_p = (width // block_width * 7 // 16) * block_width
    width_sp = (width // block_width * 8 // 16) * block_width
    n_dp, firsts, ends, ids, own_first, own_count = plan(row_counts, own_dp, own_mp)
    units = rows // UNIT
    kept_units = units // 2 - 1
    numbers = jnp.arange(kept_units, dtype=jnp.int32) * n_dp + own_dp
    source_of = jnp.sum((ends[None, :] <= numbers[:, None]).astype(jnp.int32), axis=1)
    back = jnp.clip((firsts + (own_dp - firsts) % n_dp) // n_dp, 0, kept_units - 1)
    send = jnp.minimum((ids - own_first) % n_dp + 1, units - 1)
    restore = (own_first + jnp.arange(units, dtype=jnp.int32) - 1) % n_dp
    index_own = (gate_index, up_index, down_index)
    index_both = shift(jnp.stack(index_own), dc=1)
    index_other = (index_both[0], index_both[1], index_both[2])
    weights_own = (gate_blocks, up_blocks, down_blocks)
    weights_other = tuple(shift(w, dc=1) for w in weights_own)
    still = gather_z_first(tokens[:UNIT])
    rolled, = copy_units([tokens], send, [width])
    spread = lax.all_to_all(rolled, "dp", split_axis=0, concat_axis=0, tiled=True)
    kept = kept_units * UNIT
    part_p, part_q = copy_units([spread], source_of, [width_p, width - width_p])
    gathered_parts = [
        (gather_z_first(part_p), kept, 0, 0), (gather_x_first(part_q), kept, 0, width_p), (still, UNIT, 8 * kept, 0)
    ]
    sent_parts = [
        (Z_LAST, kept, 0, 0, width_sp),
        (Z_FIRST, kept, 0, width_sp, width - width_sp),
        (Z_LAST_DIRECT, UNIT, 8 * kept, 0, width),
    ]
    sums_p, sums_q, sums_still = run_layer(
        gathered_parts, sent_parts, width, index_own, index_other, weights_own, weights_other)
    part_p = scatter_z_last(sums_p)
    part_q = scatter_z_first(sums_q)
    returned, = copy_units([part_p, part_q], back, [width])
    received = lax.all_to_all(returned, "dp", split_axis=0, concat_axis=0, tiled=True)
    still = scatter_z_last_direct(sums_still)
    restored, = copy_units([received], restore, [width], still, own_count + 1)
    return restored


def solution(mesh):
    in_specs = (
        P(("dp", "mp"), None),
        P(),
        P("mp", None, None, None),
        P("mp", None),
        P("mp", None, None, None),
        P("mp", None),
        P("mp", None, None, None),
        P("mp", None),
    )
    out_specs = P(("dp", "mp"), None)
    return jax.shard_map(run, mesh=mesh, in_specs=in_specs, out_specs=out_specs, check_vma=False)
```

```python
import functools

import jax
import jax.numpy as jnp
from jax import lax
from jax.experimental import pallas as pl
from jax.experimental.pallas import tpu as pltpu
from jax.sharding import PartitionSpec as P


NX = 4
MP = [(x, z, c) for x in range(NX) for z in range(2) for c in range(2)]


def mp_index(x, z, c):
    return (x % NX) * 4 + (z % 2) * 2 + (c % 2)


def shift_pairs(dx, dz, dc):
    return [(mp_index(x, z, c), mp_index(x + dx, z + dz, c + dc)) for x, z, c in MP]


def shift(value, dx=0, dz=0, dc=0):
    return lax.ppermute(value, "mp", shift_pairs(dx, dz, dc))


ORDER = [(dx, dz) for dx in range(NX) for dz in range(2)]


def gather_z_first(part):
    cross = shift(part, dz=1)
    pair = jnp.concatenate([part, cross], axis=0)
    left = shift(pair, dx=1)
    right = shift(pair, dx=-1)
    far = shift(pair, dx=2)
    return [(pair, [(0, 0), (0, 1)]), (left, [(3, 0), (3, 1)]), (right, [(1, 0), (1, 1)]), (far, [(2, 0), (2, 1)])]


def gather_x_first(part):
    left = shift(part, dx=1)
    right = shift(part, dx=-1)
    far = shift(part, dx=2)
    cross = shift(part, dz=1)
    three = jnp.concatenate([left, right, far], axis=0)
    three_cross = shift(three, dz=1)
    return [(part, [(0, 0)]), (three, [(3, 0), (1, 0), (2, 0)]),
            (cross, [(0, 1)]), (three_cross, [(3, 1), (1, 1), (2, 1)])]


Z_LAST = [[(2, 0)], [(2, 1)], [(1, 0)], [(1, 1)], [(3, 0)], [(3, 1)], [(0, 0)], [(0, 1)]]
Z_LAST_DIRECT = [[(dx, 0), (dx, 1)] for dx in (2, 1, 3, 0)]
Z_FIRST = [[(dx, 1) for dx in range(NX)], [(dx, 0) for dx in range(NX)]]


def layer_kernel(loads, stores, nonzero, own_columns,
                 gate_index, up_index, down_index,
                 gate_own, gate_other, up_own, up_other, down_own, down_other, *rest):
    n_in, n_out = 1 + max(p[0] for p in loads), 1 + max(p[0] for p in stores)
    pieces, outs = rest[:n_in], rest[n_in:n_in + n_out]
    x_all, gate_left, up_left, total = rest[n_in + n_out:]
    step = pl.program_id(0)
    block_width = gate_own.shape[2]
    unit_width = gate_own.shape[3]

    @pl.when(step == 0)
    def _():
        for which, piece_row, rows, row, column, width in loads:
            x_all[row:row + rows, column:column + width] = pieces[which][piece_row:piece_row + rows, :]
        total[...] = jnp.zeros_like(total)

    def run(gate_ref, up_ref, down_ref):
        def project(index, weights, left):
            for k in range(nonzero):
                at = pl.multiple_of(index[step, k] * block_width, block_width)
                left[:, k * block_width:(k + 1) * block_width] = x_all[:, pl.ds(at, block_width)]
            return jnp.dot(left[...], weights[0].reshape(nonzero * block_width, unit_width),
                           preferred_element_type=jnp.float32)

        gate = project(gate_index, gate_ref, gate_left)
        up = project(up_index, up_ref, up_left)
        hidden = (gate / (1.0 + jnp.exp(-gate)) * up).astype(jnp.bfloat16)
        for k in range(0, nonzero, 2):
            pair = jnp.concatenate([down_ref[0, k], down_ref[0, k + 1]], axis=1)
            value = jnp.dot(hidden, pair, preferred_element_type=jnp.float32)
            for i in range(2):
                at = pl.multiple_of(down_index[step, k + i] * block_width, block_width)
                total[:, pl.ds(at, block_width)] += value[:, i * block_width:(i + 1) * block_width]

    @pl.when(step < own_columns)
    def _():
        run(gate_own, up_own, down_own)

    @pl.when(step >= own_columns)
    def _():
        run(gate_other, up_other, down_other)

    @pl.when(step == 2 * own_columns - 1)
    def _():
        for which, out_row, rows, row, column, width in stores:
            outs[which][out_row:out_row + rows, :] = total[row:row + rows, column:column + width].astype(jnp.bfloat16)


def run_layer(gathered_parts, sent_parts, width, index_own, index_other, weights_own, weights_other):
    loads, stores, pieces, out_shapes, all_rows = [], [], [], [], 0
    for gathered, rows, row, column in gathered_parts:
        all_rows = max(all_rows, row + 8 * rows)
        for array, keys in gathered:
            for i, key in enumerate(keys):
                loads.append((len(pieces), i * rows, rows, row + ORDER.index(key) * rows, column, array.shape[1]))
            pieces.append(array)
    for sends, rows, row, column, part_width in sent_parts:
        for keys in sends:
            for i, key in enumerate(keys):
                stores.append((len(out_shapes), i * rows, rows, row + ORDER.index(key) * rows, column, part_width))
            out_shapes.append((len(keys) * rows, part_width))
    own_columns, nonzero, block_width, _ = weights_own[0].shape
    tables = [jnp.concatenate([a, b], axis=0) for a, b in zip(index_own, index_other)]

    def own_map(j, *_):
        return (jnp.minimum(j, own_columns - 1), 0, 0, 0)

    def other_map(j, *_):
        return (jnp.maximum(j - own_columns, 0), 0, 0, 0)

    weight_specs, weights = [], []
    for own, other in zip(weights_own, weights_other):
        shape = (1,) + own.shape[1:]
        weight_specs += [pl.BlockSpec(shape, own_map), pl.BlockSpec(shape, other_map)]
        weights += [own, other]
    sums = pl.pallas_call(
        functools.partial(layer_kernel, loads, stores, nonzero, own_columns),
        grid_spec=pltpu.PrefetchScalarGridSpec(
            num_scalar_prefetch=3,
            grid=(2 * own_columns,),
            in_specs=weight_specs + [pl.BlockSpec(memory_space=pltpu.VMEM)] * len(pieces),
            out_specs=[pl.BlockSpec(memory_space=pltpu.VMEM)] * len(out_shapes),
            scratch_shapes=[
                pltpu.VMEM((all_rows, width), jnp.bfloat16),
                pltpu.VMEM((all_rows, nonzero * block_width), jnp.bfloat16),
                pltpu.VMEM((all_rows, nonzero * block_width), jnp.bfloat16),
                pltpu.VMEM((all_rows, width), jnp.float32),
            ],
        ),
        out_shape=[jax.ShapeDtypeStruct(s, jnp.bfloat16) for s in out_shapes],
        compiler_params=pltpu.CompilerParams(
            dimension_semantics=("arbitrary",), vmem_limit_bytes=45 * 1024 * 1024),
        name="sparse_ffn",
    )(*tables, *weights, *pieces)
    split, at = [], 0
    for sends, *_ in sent_parts:
        split.append(sums[at:at + len(sends)])
        at += len(sends)
    return split


def wide(value):
    return value.astype(jnp.float32)


def narrow(value):
    return value.astype(jnp.bfloat16)


def scatter_z_last(sums):
    far_0, far_1, next_10, next_11, next_30, next_31, own_0, own_1 = sums
    got_0 = shift(far_0, dx=1)
    got_1 = shift(far_1, dx=-1)
    left_1 = shift(next_11, dx=1)
    right_0 = shift(next_30, dx=-1)
    left_0 = shift(narrow(wide(next_10) + wide(got_0)), dx=1)
    right_1 = shift(narrow(wide(next_31) + wide(got_1)), dx=-1)
    got_z = shift(narrow(wide(own_1) + wide(left_1) + wide(right_1)), dz=1)
    return narrow(wide(own_0) + wide(left_0) + wide(right_0) + wide(got_z))


def scatter_z_last_direct(sums):
    far, next_1, next_3, own = sums
    rows = far.shape[0] // 2
    got = [shift(far, dx=2), shift(next_1, dx=1), shift(next_3, dx=-1)]
    met = wide(own) + wide(got[0]) + wide(got[1]) + wide(got[2])
    got_z = shift(narrow(met[rows:]), dz=1)
    return narrow(met[:rows] + wide(got_z))


def scatter_z_first(sums):
    cross_1, cross_0 = sums
    rows = cross_1.shape[0] // NX
    got_cross = shift(cross_1, dz=1)
    met = [wide(cross_0[i * rows:(i + 1) * rows]) + wide(got_cross[i * rows:(i + 1) * rows]) for i in range(NX)]
    return narrow(met[0] + wide(shift(narrow(met[1]), dx=1))
                  + wide(shift(narrow(met[3]), dx=-1))
                  + wide(shift(narrow(met[2]), dx=2)))


UNIT = 8


def copy_units(sources, index, out_widths, head=None, count=None):
    units = index.shape[0]
    in_starts = [sum(s.shape[1] for s in sources[:i]) for i in range(len(sources))]
    out_starts = [sum(out_widths[:i]) for i in range(len(out_widths))]
    spans = []
    for i, source in enumerate(sources):
        for o, width in enumerate(out_widths):
            low = max(in_starts[i], out_starts[o])
            high = min(in_starts[i] + source.shape[1], out_starts[o] + width)
            if low < high:
                spans.append((i, low - in_starts[i], o, low - out_starts[o], high - low))
    ins_all = list(sources) if head is None else [*sources, head]
    table = index if head is None else jnp.concatenate([index, count[None]])

    def kernel(table, *refs):
        ins, outs = refs[:len(sources)], refs[len(ins_all):]
        for unit in range(units):
            start = pl.multiple_of(table[unit] * UNIT, UNIT)
            for i, from_column, o, to_column, width in spans:
                if head is not None and unit == 0:
                    value = refs[len(sources)][...]
                else:
                    value = ins[i][pl.ds(start, UNIT), from_column:from_column + width]
                    if head is not None:
                        value = jnp.where(unit < table[units], value, jnp.zeros_like(value))
                outs[o][unit * UNIT:(unit + 1) * UNIT, to_column:to_column + width] = value

    return pl.pallas_call(
        kernel,
        in_specs=[pl.BlockSpec(memory_space=pltpu.SMEM)] + [pl.BlockSpec(memory_space=pltpu.VMEM)] * len(ins_all),
        out_specs=[pl.BlockSpec(memory_space=pltpu.VMEM)] * len(out_widths),
        out_shape=[jax.ShapeDtypeStruct((units * UNIT, w), jnp.bfloat16) for w in out_widths],
        compiler_params=pltpu.CompilerParams(vmem_limit_bytes=8 * 1024 * 1024),
        name="copy_units",
    )(table, *ins_all)


def plan(row_counts, own_dp, own_mp):
    n_dp = row_counts.shape[0]
    counts = lax.dynamic_slice_in_dim(row_counts, own_mp, 1, axis=1)[:, 0] // UNIT - 1
    ends = jnp.cumsum(counts)
    firsts = ends - counts
    ids = jnp.arange(n_dp, dtype=jnp.int32)
    own_first = lax.dynamic_index_in_dim(firsts, own_dp, keepdims=False)
    own_count = lax.dynamic_index_in_dim(counts, own_dp, keepdims=False)
    return n_dp, firsts, ends, ids, own_first, own_count


def run(tokens, row_counts, gate_blocks, gate_index, up_blocks, up_index, down_blocks, down_index):
    own_dp = lax.axis_index("dp")
    own_mp = lax.axis_index("mp")
    rows, width = tokens.shape
    block_width = gate_blocks.shape[2]
    width_p = (width // block_width * 7 // 16) * block_width
    width_sp = (width // block_width * 9 // 16) * block_width
    n_dp, firsts, ends, ids, own_first, own_count = plan(row_counts, own_dp, own_mp)
    units = rows // UNIT
    kept_units = units // 2 - 1
    numbers = jnp.arange(kept_units, dtype=jnp.int32) * n_dp + own_dp
    source_of = jnp.sum((ends[None, :] <= numbers[:, None]).astype(jnp.int32), axis=1)
    back = jnp.clip((firsts + (own_dp - firsts) % n_dp) // n_dp, 0, kept_units - 1)
    send = jnp.minimum((ids - own_first) % n_dp + 1, units - 1)
    restore = (own_first + jnp.arange(units, dtype=jnp.int32) - 1) % n_dp
    index_own = (gate_index, up_index, down_index)
    index_both = shift(jnp.stack(index_own), dc=1)
    index_other = (index_both[0], index_both[1], index_both[2])
    weights_own = (gate_blocks, up_blocks, down_blocks)
    weights_other = tuple(shift(w, dc=1) for w in weights_own)
    still = gather_z_first(tokens[:UNIT])
    rolled, = copy_units([tokens], send, [width])
    spread = lax.all_to_all(rolled, "dp", split_axis=0, concat_axis=0, tiled=True)
    kept = kept_units * UNIT
    part_p, part_q = copy_units([spread], source_of, [width_p, width - width_p])
    gathered_parts = [
        (gather_z_first(part_p), kept, 0, 0), (gather_x_first(part_q), kept, 0, width_p), (still, UNIT, 8 * kept, 0)
    ]
    sent_parts = [
        (Z_LAST, kept, 0, 0, width_sp),
        (Z_FIRST, kept, 0, width_sp, width - width_sp),
        (Z_LAST_DIRECT, UNIT, 8 * kept, 0, width),
    ]
    sums_p, sums_q, sums_still = run_layer(
        gathered_parts, sent_parts, width, index_own, index_other, weights_own, weights_other)
    part_p = scatter_z_last(sums_p)
    part_q = scatter_z_first(sums_q)
    returned, = copy_units([part_p, part_q], back, [width])
    received = lax.all_to_all(returned, "dp", split_axis=0, concat_axis=0, tiled=True)
    still = scatter_z_last_direct(sums_still)
    restored, = copy_units([received], restore, [width], still, own_count + 1)
    return restored


def solution(mesh):
    in_specs = (
        P(("dp", "mp"), None),
        P(),
        P("mp", None, None, None),
        P("mp", None),
        P("mp", None, None, None),
        P("mp", None),
        P("mp", None, None, None),
        P("mp", None),
    )
    out_specs = P(("dp", "mp"), None)
    return jax.shard_map(run, mesh=mesh, in_specs=in_specs, out_specs=out_specs, check_vma=False)
```

```python
import functools

import jax
import jax.numpy as jnp
from jax import lax
from jax.experimental import pallas as pl
from jax.experimental.pallas import tpu as pltpu
from jax.sharding import PartitionSpec as P


NX = 4
MP = [(x, z, c) for x in range(NX) for z in range(2) for c in range(2)]


def mp_index(x, z, c):
    return (x % NX) * 4 + (z % 2) * 2 + (c % 2)


def shift_pairs(dx, dz, dc):
    return [(mp_index(x, z, c), mp_index(x + dx, z + dz, c + dc)) for x, z, c in MP]


def shift(value, dx=0, dz=0, dc=0):
    return lax.ppermute(value, "mp", shift_pairs(dx, dz, dc))


ORDER = [(dx, dz) for dx in range(NX) for dz in range(2)]


def gather_z_first(part):
    cross = shift(part, dz=1)
    pair = jnp.concatenate([part, cross], axis=0)
    left = shift(pair, dx=1)
    right = shift(pair, dx=-1)
    far = shift(pair, dx=2)
    return [(pair, [(0, 0), (0, 1)]), (left, [(3, 0), (3, 1)]), (right, [(1, 0), (1, 1)]), (far, [(2, 0), (2, 1)])]


def gather_x_first(part):
    left = shift(part, dx=1)
    right = shift(part, dx=-1)
    far = shift(part, dx=2)
    cross = shift(part, dz=1)
    three = jnp.concatenate([left, right, far], axis=0)
    three_cross = shift(three, dz=1)
    return [(part, [(0, 0)]), (three, [(3, 0), (1, 0), (2, 0)]),
            (cross, [(0, 1)]), (three_cross, [(3, 1), (1, 1), (2, 1)])]


Z_LAST = [[(2, 0)], [(2, 1)], [(1, 0)], [(1, 1)], [(3, 0)], [(3, 1)], [(0, 0)], [(0, 1)]]
Z_FIRST = [[(dx, 1) for dx in range(NX)], [(dx, 0) for dx in range(NX)]]


def layer_kernel(loads, stores, nonzero, own_columns,
                 gate_index, up_index, down_index,
                 gate_own, gate_other, up_own, up_other, down_own, down_other, *rest):
    n_in, n_out = 1 + max(p[0] for p in loads), 1 + max(p[0] for p in stores)
    pieces, outs = rest[:n_in], rest[n_in:n_in + n_out]
    x_all, gate_left, up_left, total = rest[n_in + n_out:]
    step = pl.program_id(0)
    block_width = gate_own.shape[2]
    unit_width = gate_own.shape[3]

    @pl.when(step == 0)
    def _():
        for which, piece_row, rows, row, column, width in loads:
            x_all[row:row + rows, column:column + width] = pieces[which][piece_row:piece_row + rows, :]
        total[...] = jnp.zeros_like(total)

    def run(gate_ref, up_ref, down_ref):
        def project(index, weights, left):
            for k in range(nonzero):
                at = pl.multiple_of(index[step, k] * block_width, block_width)
                left[:, k * block_width:(k + 1) * block_width] = x_all[:, pl.ds(at, block_width)]
            return jnp.dot(left[...], weights[0].reshape(nonzero * block_width, unit_width),
                           preferred_element_type=jnp.float32)

        gate = project(gate_index, gate_ref, gate_left)
        up = project(up_index, up_ref, up_left)
        hidden = (gate / (1.0 + jnp.exp(-gate)) * up).astype(jnp.bfloat16)
        for k in range(0, nonzero, 2):
            pair = jnp.concatenate([down_ref[0, k], down_ref[0, k + 1]], axis=1)
            value = jnp.dot(hidden, pair, preferred_element_type=jnp.float32)
            for i in range(2):
                at = pl.multiple_of(down_index[step, k + i] * block_width, block_width)
                total[:, pl.ds(at, block_width)] += value[:, i * block_width:(i + 1) * block_width]

    @pl.when(step < own_columns)
    def _():
        run(gate_own, up_own, down_own)

    @pl.when(step >= own_columns)
    def _():
        run(gate_other, up_other, down_other)

    @pl.when(step == 2 * own_columns - 1)
    def _():
        for which, out_row, rows, row, column, width in stores:
            outs[which][out_row:out_row + rows, :] = total[row:row + rows, column:column + width].astype(jnp.bfloat16)


def run_layer(gathered_parts, sent_parts, width, index_own, index_other, weights_own, weights_other):
    loads, stores, pieces, out_shapes, all_rows = [], [], [], [], 0
    for gathered, rows, row, column in gathered_parts:
        all_rows = max(all_rows, row + 8 * rows)
        for array, keys in gathered:
            for i, key in enumerate(keys):
                loads.append((len(pieces), i * rows, rows, row + ORDER.index(key) * rows, column, array.shape[1]))
            pieces.append(array)
    for sends, rows, row, column, part_width in sent_parts:
        for keys in sends:
            for i, key in enumerate(keys):
                stores.append((len(out_shapes), i * rows, rows, row + ORDER.index(key) * rows, column, part_width))
            out_shapes.append((len(keys) * rows, part_width))
    own_columns, nonzero, block_width, _ = weights_own[0].shape
    tables = [jnp.concatenate([a, b], axis=0) for a, b in zip(index_own, index_other)]

    def own_map(j, *_):
        return (jnp.minimum(j, own_columns - 1), 0, 0, 0)

    def other_map(j, *_):
        return (jnp.maximum(j - own_columns, 0), 0, 0, 0)

    weight_specs, weights = [], []
    for own, other in zip(weights_own, weights_other):
        shape = (1,) + own.shape[1:]
        weight_specs += [pl.BlockSpec(shape, own_map), pl.BlockSpec(shape, other_map)]
        weights += [own, other]
    sums = pl.pallas_call(
        functools.partial(layer_kernel, loads, stores, nonzero, own_columns),
        grid_spec=pltpu.PrefetchScalarGridSpec(
            num_scalar_prefetch=3,
            grid=(2 * own_columns,),
            in_specs=weight_specs + [pl.BlockSpec(memory_space=pltpu.VMEM)] * len(pieces),
            out_specs=[pl.BlockSpec(memory_space=pltpu.VMEM)] * len(out_shapes),
            scratch_shapes=[
                pltpu.VMEM((all_rows, width), jnp.bfloat16),
                pltpu.VMEM((all_rows, nonzero * block_width), jnp.bfloat16),
                pltpu.VMEM((all_rows, nonzero * block_width), jnp.bfloat16),
                pltpu.VMEM((all_rows, width), jnp.float32),
            ],
        ),
        out_shape=[jax.ShapeDtypeStruct(s, jnp.bfloat16) for s in out_shapes],
        compiler_params=pltpu.CompilerParams(
            dimension_semantics=("arbitrary",), vmem_limit_bytes=45 * 1024 * 1024),
        name="sparse_ffn",
    )(*tables, *weights, *pieces)
    split, at = [], 0
    for sends, *_ in sent_parts:
        split.append(sums[at:at + len(sends)])
        at += len(sends)
    return split


def wide(value):
    return value.astype(jnp.float32)


def narrow(value):
    return value.astype(jnp.bfloat16)


def scatter_z_last(sums):
    far_0, far_1, next_10, next_11, next_30, next_31, own_0, own_1 = sums
    got_0 = shift(far_0, dx=1)
    got_1 = shift(far_1, dx=-1)
    left_1 = shift(next_11, dx=1)
    right_0 = shift(next_30, dx=-1)
    left_0 = shift(narrow(wide(next_10) + wide(got_0)), dx=1)
    right_1 = shift(narrow(wide(next_31) + wide(got_1)), dx=-1)
    got_z = shift(narrow(wide(own_1) + wide(left_1) + wide(right_1)), dz=1)
    return narrow(wide(own_0) + wide(left_0) + wide(right_0) + wide(got_z))


def scatter_z_last_direct(sums):
    far_0, far_1, next_10, next_11, next_30, next_31, own_0, own_1 = sums

    def meet(own, next_1, next_3, far):
        got = [shift(next_1, dx=1), shift(next_3, dx=-1),
               shift(far, dx=2)]
        return wide(own) + wide(got[0]) + wide(got[1]) + wide(got[2])

    crossing = narrow(meet(own_1, next_11, next_31, far_1))
    got_z = shift(crossing, dz=1)
    return narrow(meet(own_0, next_10, next_30, far_0) + wide(got_z))


def scatter_z_first(sums):
    cross_1, cross_0 = sums
    rows = cross_1.shape[0] // NX
    got_cross = shift(cross_1, dz=1)
    met = [wide(cross_0[i * rows:(i + 1) * rows]) + wide(got_cross[i * rows:(i + 1) * rows]) for i in range(NX)]
    return narrow(met[0] + wide(shift(narrow(met[1]), dx=1))
                  + wide(shift(narrow(met[3]), dx=-1))
                  + wide(shift(narrow(met[2]), dx=2)))


UNIT = 8


def copy_units(sources, index, out_widths, head=None, count=None):
    units = index.shape[0]
    in_starts = [sum(s.shape[1] for s in sources[:i]) for i in range(len(sources))]
    out_starts = [sum(out_widths[:i]) for i in range(len(out_widths))]
    spans = []
    for i, source in enumerate(sources):
        for o, width in enumerate(out_widths):
            low = max(in_starts[i], out_starts[o])
            high = min(in_starts[i] + source.shape[1], out_starts[o] + width)
            if low < high:
                spans.append((i, low - in_starts[i], o, low - out_starts[o], high - low))
    ins_all = list(sources) if head is None else [*sources, head]
    table = index if head is None else jnp.concatenate([index, count[None]])

    def kernel(table, *refs):
        ins, outs = refs[:len(sources)], refs[len(ins_all):]
        for unit in range(units):
            start = pl.multiple_of(table[unit] * UNIT, UNIT)
            for i, from_column, o, to_column, width in spans:
                if head is not None and unit == 0:
                    value = refs[len(sources)][...]
                else:
                    value = ins[i][pl.ds(start, UNIT), from_column:from_column + width]
                    if head is not None:
                        value = jnp.where(unit < table[units], value, jnp.zeros_like(value))
                outs[o][unit * UNIT:(unit + 1) * UNIT, to_column:to_column + width] = value

    return pl.pallas_call(
        kernel,
        in_specs=[pl.BlockSpec(memory_space=pltpu.SMEM)] + [pl.BlockSpec(memory_space=pltpu.VMEM)] * len(ins_all),
        out_specs=[pl.BlockSpec(memory_space=pltpu.VMEM)] * len(out_widths),
        out_shape=[jax.ShapeDtypeStruct((units * UNIT, w), jnp.bfloat16) for w in out_widths],
        compiler_params=pltpu.CompilerParams(vmem_limit_bytes=8 * 1024 * 1024),
        name="copy_units",
    )(table, *ins_all)


def plan(row_counts, own_dp, own_mp):
    n_dp = row_counts.shape[0]
    counts = lax.dynamic_slice_in_dim(row_counts, own_mp, 1, axis=1)[:, 0] // UNIT - 1
    ends = jnp.cumsum(counts)
    firsts = ends - counts
    ids = jnp.arange(n_dp, dtype=jnp.int32)
    own_first = lax.dynamic_index_in_dim(firsts, own_dp, keepdims=False)
    own_count = lax.dynamic_index_in_dim(counts, own_dp, keepdims=False)
    return n_dp, firsts, ends, ids, own_first, own_count


def run(tokens, row_counts, gate_blocks, gate_index, up_blocks, up_index, down_blocks, down_index):
    own_dp = lax.axis_index("dp")
    own_mp = lax.axis_index("mp")
    rows, width = tokens.shape
    block_width = gate_blocks.shape[2]
    width_p = (width // block_width * 7 // 16) * block_width
    width_sp = (width // block_width * 9 // 16) * block_width
    n_dp, firsts, ends, ids, own_first, own_count = plan(row_counts, own_dp, own_mp)
    units = rows // UNIT
    kept_units = units // 2 - 1
    numbers = jnp.arange(kept_units, dtype=jnp.int32) * n_dp + own_dp
    source_of = jnp.sum((ends[None, :] <= numbers[:, None]).astype(jnp.int32), axis=1)
    back = jnp.clip((firsts + (own_dp - firsts) % n_dp) // n_dp, 0, kept_units - 1)
    send = jnp.minimum((ids - own_first) % n_dp + 1, units - 1)
    restore = (own_first + jnp.arange(units, dtype=jnp.int32) - 1) % n_dp
    index_own = (gate_index, up_index, down_index)
    index_both = shift(jnp.stack(index_own), dc=1)
    index_other = (index_both[0], index_both[1], index_both[2])
    weights_own = (gate_blocks, up_blocks, down_blocks)
    weights_other = tuple(shift(w, dc=1) for w in weights_own)
    still = gather_z_first(tokens[:UNIT])
    rolled, = copy_units([tokens], send, [width])
    spread = lax.all_to_all(rolled, "dp", split_axis=0, concat_axis=0, tiled=True)
    kept = kept_units * UNIT
    part_p, part_q = copy_units([spread], source_of, [width_p, width - width_p])
    gathered_parts = [
        (gather_z_first(part_p), kept, 0, 0), (gather_x_first(part_q), kept, 0, width_p), (still, UNIT, 8 * kept, 0)
    ]
    sent_parts = [
        (Z_LAST, kept, 0, 0, width_sp),
        (Z_FIRST, kept, 0, width_sp, width - width_sp),
        (Z_LAST, UNIT, 8 * kept, 0, width),
    ]
    sums_p, sums_q, sums_still = run_layer(
        gathered_parts, sent_parts, width, index_own, index_other, weights_own, weights_other)
    part_p = scatter_z_last(sums_p)
    part_q = scatter_z_first(sums_q)
    returned, = copy_units([part_p, part_q], back, [width])
    received = lax.all_to_all(returned, "dp", split_axis=0, concat_axis=0, tiled=True)
    still = scatter_z_last_direct(sums_still)
    restored, = copy_units([received], restore, [width], still, own_count + 1)
    return restored


def solution(mesh):
    in_specs = (
        P(("dp", "mp"), None),
        P(),
        P("mp", None, None, None),
        P("mp", None),
        P("mp", None, None, None),
        P("mp", None),
        P("mp", None, None, None),
        P("mp", None),
    )
    out_specs = P(("dp", "mp"), None)
    return jax.shard_map(run, mesh=mesh, in_specs=in_specs, out_specs=out_specs, check_vma=False)
```
